1024 devices in a mesh: len: 8 (over x, core), brick: 128 (over z, y).
Axes of the slice: x: 4, y: 8, z: 16, core: 2. Of those that a mesh axis runs over, the one named last changes fastest.
Arguments:
- forces: float32 [3, 64, 2048, 128], P(None, 'len', 'brick'), may hold values from -6 to 6
- modulus: float32 [64, 2048, 128], P('len', 'brick'), may hold values from 1 to 10
- occupancy: int32 [64, 2048, 128], P('len', 'brick'), may hold values 0 or 1
- bonded: int32 [64, 2048, 128], P('len', 'brick'), may hold values 0 or 1
Outputs:
- solution: float32 [3, 64, 2048, 128], P(None, 'len', 'brick')
The draws below stay inside these ranges and needn't reach their ends.
All inputs are finite; a program needn't handle non-finite values. No bound on the sum of `occupancy` or of `bonded` on one device may be relied on, other than what follows from the above.
Results may differ from the reference program's by a relative error of at most 0.0001.
Values sent between devices are 32-bit elements; how exact they have to be, the bound alone decides.
A program may use at most 64 MiB of HBM per device.

```python
import math
import jax
import jax.numpy as jnp
from jax import lax

CZ = 128
LEVELS = 3
PRE_SWEEPS = 2
POST_SWEEPS = 2
COARSE_SWEEPS = 4
NX = 64
NY = 2048


def place_ends(values, rng, low, largest):
    index_at = [jax.random.randint(jax.random.fold_in(rng, axis), (), 0, length) for axis, length in enumerate(values.shape)]
    longest = values.shape.index(max(values.shape))
    beside = index_at[:longest] + [(index_at[longest] + 1) % values.shape[longest]] + index_at[longest + 1:]
    return values.at[tuple(index_at)].set(low).at[tuple(beside)].set(largest)


def level_of(stream_key, shape, cuts, low, high):
    loudness, own = 1.0, jax.random.fold_in(stream_key, 6)
    for position, shards_of in cuts:
        heights = jnp.exp(jax.random.uniform(jax.random.fold_in(own, position), (shards_of,), jnp.float32, low / len(cuts), high / len(cuts)))
        loudness = loudness * jnp.repeat(heights, shape[position] // shards_of).reshape([-1 if axis == position else 1 for axis in range(len(shape))])
    return loudness


def gaussian(stream_key, dims, deviation, reach, shards=(), dtype=jnp.bfloat16):
    factor_of = level_of(stream_key, dims, shards, -0.22, 0.18) if shards else 1.0
    drawn = jax.random.normal(stream_key, dims, jnp.float32) * deviation * factor_of
    return jnp.minimum(jnp.maximum(drawn, -reach), reach).astype(dtype)


def setup_inputs(seed: int = 0) -> dict:
    keys = jax.random.split(jax.random.key(seed), 5)
    return {
        "forces": gaussian(keys[0], (3, NX, NY, CZ), 1.0, 6.0, ((1, 8), (2, 128)), jnp.float32),
        "modulus": jnp.clip(jnp.exp(math.log(10.0) - 2.3025851 * jax.random.uniform(keys[1], (NX, NY, CZ), jnp.float32) ** level_of(keys[1], (NX, NY, CZ), ((0, 8), (1, 128)), -0.2, 0.2)), 1.0, 10.0),
        "occupancy": place_ends((jax.random.randint(keys[2], (NX, NY, CZ), 0, 4) < 3).astype(jnp.int32), jax.random.fold_in(keys[2], 1), 0, 1),
        "bonded": place_ends((jax.random.randint(keys[3], (NX, NY, CZ), 0, 16) < 1).astype(jnp.int32), jax.random.fold_in(keys[3], 1), 0, 1),
    }


DAMPING = 0.6
COUPLING = 0.2
MASS_TERM = 0.1
PENALTY = 20.0
COARSE_SCALE = 0.25


def smooth(extended):
    ndims = extended.ndim
    padded = jnp.pad(extended, [(0, 0)] * (ndims - 1) + [(1, 1)])
    depth = padded.shape[-1]
    total = extended + 0.5 * (lax.slice_in_dim(padded, 0, depth - 2, axis=ndims - 1) + lax.slice_in_dim(padded, 2, depth, axis=ndims - 1))
    for axis_now in (ndims - 2, ndims - 3):
        extent = total.shape[axis_now]
        total = lax.slice_in_dim(total, 1, extent - 1, axis=axis_now) + 0.5 * (lax.slice_in_dim(total, 0, extent - 2, axis=axis_now) + lax.slice_in_dim(total, 2, extent, axis=axis_now))
    return total


def weights_only(coeff_ext):
    centre = coeff_ext[1:-1, 1:-1, :]
    weight_total = 6.0 * centre + smooth(coeff_ext)
    return centre, weight_total


def stencil(field_ext, coeff_ext):
    centre, weight_total = weights_only(coeff_ext)
    field_mid = field_ext[:, 1:-1, 1:-1, :]
    product_ext = coeff_ext[None] * field_ext
    product_mid = product_ext[:, 1:-1, 1:-1, :]
    gathered_sum = centre * (smooth(field_ext) - field_mid) + smooth(product_ext) - product_mid
    return centre, weight_total, gathered_sum


def apply_operator(field_ext, coeff_ext, shift_term):
    centre, weight_total, gathered_sum = stencil(field_ext, coeff_ext)
    field_mid = field_ext[:, 1:-1, 1:-1, :]
    return (weight_total + shift_term) * field_mid - gathered_sum + COUPLING * centre * jnp.sum(field_mid, axis=0)


def jacobi_step(field_ext, coeff_ext, shift_term, source, extra):
    centre, weight_total, gathered_sum = stencil(field_ext, coeff_ext)
    field_mid = field_ext[:, 1:-1, 1:-1, :]
    applied = (weight_total + shift_term) * field_mid - gathered_sum + COUPLING * centre * jnp.sum(field_mid, axis=0)
    return field_mid + DAMPING * (source - applied) / (weight_total + shift_term + COUPLING * centre + extra)


def first_step(coeff_ext, shift_term, source):
    centre, weight_total = weights_only(coeff_ext)
    return DAMPING * source / (weight_total + shift_term + COUPLING * centre)


def restrict_field(values):
    shaped = values.reshape(values.shape[0], values.shape[1] // 2, 2, values.shape[2] // 2, 2, values.shape[3] // 2, 2)
    return jnp.mean(shaped, axis=(2, 4, 6))


def restrict_cells(values):
    return restrict_field(values[None])[0]


def prolong(values):
    return jnp.repeat(jnp.repeat(jnp.repeat(values, 2, axis=1), 2, axis=2), 2, axis=3)


def pad_field(values):
    return jnp.pad(values, ((0, 0), (1, 1), (1, 1), (0, 0)))


def pad_coeff(values):
    return jnp.pad(values, ((1, 1), (1, 1), (0, 0)))


def reference(forces, modulus, occupancy, bonded):
    coeffs = [modulus * occupancy.astype(jnp.float32)]
    shifts = [MASS_TERM + PENALTY * bonded.astype(jnp.float32)]
    for tier_index in range(LEVELS):
        coeffs.append(COARSE_SCALE * restrict_cells(coeffs[-1]))
        shifts.append(restrict_cells(shifts[-1]))

    def coarsest_solve(source):
        coeff_ext = pad_coeff(coeffs[LEVELS])
        shift_term = shifts[LEVELS]
        iterate = first_step(coeff_ext, shift_term, source)
        for repeat_idx in range(COARSE_SWEEPS - 1):
            iterate = jacobi_step(pad_field(iterate), coeff_ext, shift_term, source, 0.0)
        return iterate

    def multigrid_pass(tier_index, source):
        coeff_ext = pad_coeff(coeffs[tier_index])
        shift_term = shifts[tier_index]
        iterate = first_step(coeff_ext, shift_term, source)
        for repeat_idx in range(PRE_SWEEPS - 1):
            iterate = jacobi_step(pad_field(iterate), coeff_ext, shift_term, source, 0.0)
        residual = source - apply_operator(pad_field(iterate), coeff_ext, shift_term)
        coarse_source = restrict_field(residual)
        if tier_index + 1 == LEVELS:
            correction = coarsest_solve(coarse_source)
        else:
            correction = multigrid_pass(tier_index + 1, coarse_source)
        iterate = iterate + prolong(correction)
        for repeat_idx in range(POST_SWEEPS):
            iterate = jacobi_step(pad_field(iterate), coeff_ext, shift_term, source, 0.0)
        return iterate

    return multigrid_pass(0, forces)
```

```python
import functools

import jax
import jax.numpy as jnp
from jax import lax
from jax.experimental import pallas as pl
from jax.experimental.pallas import tpu as pltpu
from jax.sharding import PartitionSpec as P

DAMPING = 0.6
COUPLING = 0.2
MASS_TERM = 0.1
PENALTY = 20.0
COARSE_SCALE = 0.25

NL, NB = 8, 128
X0, Y0 = 8, 16
X1, Y1 = 4, 8
H = 3
R0, R1 = Y0 + 8, Y1 + 8
DEEP = 3
GB = 2 * DEEP + 1
MESH = pl.DeviceIdType.MESH
F32 = jnp.float32


def hops(dl, db):
    worst = 0
    for l in range(8):
        dx = abs((l + dl) % 8 // 2 - l // 2)
        for q in range(8):
            dy = abs((q + db) % 8 - q)
            worst = max(worst, min(dx, 4 - dx) + min(dy, 8 - dy) + abs((q + db) // 8))
    return worst


def far_first(pairs):
    return sorted(pairs, key=lambda p: -hops(*p))


NEAR = far_first([(a, b) for a in (-1, 0, 1) for b in (-1, 0, 1) if (a, b) != (0, 0)])
FAR = far_first([(a, b) for a in range(-3, 5) for b in range(-DEEP, DEEP + 1) if (a, b) != (0, 0)])
COLUMN = far_first([(0, b) for b in range(-DEEP - 1, DEEP + 2) if b])
ROW = far_first([(a, 0) for a in range(-3, 5) if a])
GREETED = NEAR + [p for p in FAR + COLUMN if p not in NEAR]
GREETED = [p for i, p in enumerate(GREETED) if p not in GREETED[:i]]


def iota(shape, dim):
    return lax.broadcasted_iota(jnp.int32, shape, dim)


def roll(x, shift, axis):
    size = x.shape[axis]
    return pltpu.roll(x, shift % size, axis % x.ndim)


def smooth_zy(v, step):
    rows = v.shape[-2]
    lane = iota((rows, 128), 1)
    low = jnp.where(lane >= step, 0.5, 0.0).astype(F32)
    high = jnp.where(lane < 128 - step, 0.5, 0.0).astype(F32)
    t = v + low * roll(v, step, -1) + high * roll(v, -step, -1)
    return t + 0.5 * (roll(t, 1, -2) + roll(t, -1, -2))


def smooth(v, step, rows=None):
    t = smooth_zy(v, step)
    if rows is not None:
        t = t[:, :rows]
    return t[1:-1] + 0.5 * (t[:-2] + t[2:])


def sweep(v, c, sides, coeffs, firsts, step, rows=None):
    keep, couple, gain = coeffs
    cut = slice(0, rows)
    mids = [f[1:-1, cut] for f in v]
    drag = COUPLING * (mids[0] + mids[1] + mids[2])
    return [
        keep * mids[k]
        + firsts[k]
        + couple * (smooth(v[k], step, rows) - drag)
        + gain * smooth(c * v[k], step, rows)
        for k in range(3)
    ]


def residual(v, c, c_mid, e_mid, source, step, rows):
    mids = [f[1:-1, :rows] for f in v]
    drag = COUPLING * (mids[0] + mids[1] + mids[2])
    return [
        source[k]
        - e_mid * mids[k]
        + c_mid * (smooth(v[k], step, rows) - drag)
        + smooth(c * v[k], step, rows)
        for k in range(3)
    ]


def swap_pairs(x, step, axis):
    index = iota(x.shape[-2:], 1 if axis in (-1, x.ndim - 1) else 0)
    return jnp.where((index // step) % 2 == 0, roll(x, -step, axis), roll(x, step, axis))


def shift_len(w, by):
    zero = jnp.zeros_like(w[:, :1])
    if by > 0:
        return jnp.concatenate([zero, w[:, :-1]], axis=1)
    return jnp.concatenate([w[:, 1:], zero], axis=1)


def neighbours_y(t, span, padded):
    lane = iota((8, 128), 1)
    up, down = roll(t, -span, -1), (roll(t, span, -1) if span != 64 else None)
    if down is None:
        down = up
    if padded:
        zero = jnp.zeros_like(t[:1])
        up_here, up_next = up, jnp.concatenate([up[1:], zero], axis=0)
        down_here, down_back = down, jnp.concatenate([zero, down[:-1]], axis=0)
    else:
        up_here, up_next = up[1:-1], up[2:]
        down_here, down_back = down[1:-1], down[:-2]
    return jnp.where(lane < 128 - span, up_here, up_next) + jnp.where(lane >= span, down_here, down_back)


def smooth_deep(v, tier, padded):
    step = 1 if tier == 2 else 2
    lane = iota((8, 128), 1)
    low = jnp.where(lane % 32 >= step, 0.5, 0.0).astype(F32)
    high = jnp.where(lane % 32 < 32 - step, 0.5, 0.0).astype(F32)
    t = v + low * roll(v, step, -1) + high * roll(v, -step, -1)
    mid = t if padded else t[1:-1]
    t = mid + 0.5 * neighbours_y(t, 32 if tier == 2 else 64, padded)
    if tier == 2:
        first = iota((8, 128), 0) % 2 == 0
        w = swap_pairs(t, 1, -2)
        beside = w + jnp.where(first, shift_len(w, 1), shift_len(w, -1))
    else:
        beside = shift_len(t, 1) + shift_len(t, -1)
    return t + 0.5 * beside


def sum_deep(v):
    u = v + roll(v, 2, -2)
    return u + roll(u, 4, -2)


def body(
    forces, modulus, occupancy, bonded, out, raw, mod_v, occ_v, bon_v, cs1, b1, v2a, v2b, first0, first1, co0, co1,
    pair, cs2, b2, sent2, co2, co3, e2, pe2, pe1,
    load_sem, send_a, recv_a, send_b, recv_b, send_k, recv_k, send_v, recv_v, send_w, recv_w,
    send_g, recv_g, send_h, recv_h, send_d, recv_d,
):
    me_l, me_b = lax.axis_index("len"), lax.axis_index("brick")

    def device(dl, db):
        return (lax.rem(me_l + dl + NL, NL), lax.rem(me_b + db + NB, NB))

    loads = [
        pltpu.make_async_copy(modulus, mod_v, load_sem.at[0]),
        pltpu.make_async_copy(occupancy, occ_v, load_sem.at[1]),
        pltpu.make_async_copy(bonded, bon_v, load_sem.at[2]),
        pltpu.make_async_copy(forces, raw.at[pl.ds(0, 3), pl.ds(H, X0), pl.ds(0, Y0), :], load_sem.at[3]),
    ]
    for load in loads:
        load.start()
    barrier = pltpu.get_barrier_semaphore()
    for dl, db in GREETED:
        pl.semaphore_signal(barrier, inc=1, device_id=device(dl, db), device_id_type=MESH)

    def exchange(buf, sends, recvs, width, size_x, size_y, rows, off):
        copies = []
        for i, (dl, db) in enumerate(NEAR):
            xs, xd, nx = {
                0: (off, off, size_x),
                1: (off + size_x - width, off - width, width),
                -1: (off, off + size_x, width),
            }[dl]
            ys, yd, ny = {
                0: (0, 0, size_y),
                1: (size_y - width, rows - width, width),
                -1: (0, size_y, width),
            }[db]
            copy = pltpu.make_async_remote_copy(
                src_ref=buf.at[:, pl.ds(xs, nx), pl.ds(ys, ny), :],
                dst_ref=buf.at[:, pl.ds(xd, nx), pl.ds(yd, ny), :],
                send_sem=sends.at[i],
                recv_sem=recvs.at[i],
                device_id=device(dl, db),
                device_id_type=MESH,
            )
            copy.start()
            copies.append(copy)
        return copies

    def arrive(copies):
        for copy in copies:
            copy.wait_recv()

    def leave(copies):
        for copy in copies:
            copy.wait_send()

    one, zero = jnp.float32(1.0), jnp.float32(0.0)
    low_x = jnp.where(me_l > 0, one, zero)
    high_x = jnp.where(me_l < NL - 1, one, zero)
    low_y = jnp.where(me_b > 0, one, zero)
    high_y = jnp.where(me_b < NB - 1, one, zero)

    def inside(n_local, halo, rows, y_local):
        row = iota((rows, 128), 0)
        in_y = jnp.where(row < y_local, one, jnp.where(row < y_local + 4, high_y, low_y))
        parts = [jnp.broadcast_to((in_y * low_x)[None], (halo, rows, 128))]
        parts.append(jnp.broadcast_to(in_y[None], (n_local, rows, 128)))
        parts.append(jnp.broadcast_to((in_y * high_x)[None], (halo, rows, 128)))
        return jnp.concatenate(parts, axis=0)

    for load in loads[:3]:
        load.wait()
    c_here = mod_v[...] * occ_v[...].astype(F32)
    s_here = MASS_TERM + PENALTY * bon_v[...].astype(F32)
    raw[3, H : H + X0, 0:Y0, :] = s_here
    raw[4, H : H + X0, 0:Y0, :] = c_here
    loads[3].wait()
    pl.semaphore_wait(barrier, len(GREETED))
    copies_a = exchange(raw, send_a, recv_a, H, X0, Y0, R0, H)

    def halve(fields):
        result = []
        for k, f in enumerate(fields):
            f = f.reshape(X1, 2, Y0, 128)
            pair[k] = f[:, 0] + f[:, 1]
            u = pair[k, :, pl.ds(0, Y1, stride=2), :] + pair[k, :, pl.ds(1, Y1, stride=2), :]
            result.append(0.125 * (u + swap_pairs(u, 1, -1)))
        return result

    def flatten(fields):
        stacked = [f.reshape(2, 2, Y1, 128) for f in fields]
        stacked = jnp.concatenate([f[:, 0] + f[:, 1] for f in stacked], axis=0)
        n = stacked.shape[0]
        a, b = iota((128, 128), 0), iota((128, 128), 1)
        squeeze = jnp.where(a // 4 == b % 32, 0.0625, 0.0).astype(F32)
        t = jnp.dot(
            stacked.reshape(n * 8, 128), squeeze, precision=lax.Precision.HIGHEST, preferred_element_type=F32
        ).reshape(n, 8, 128)
        t = jnp.where(iota((8, 128), 1) // 32 == iota((8, 128), 0) // 2, t, 0.0)
        t = t + roll(t, 4, -2)
        t = t + roll(t, 2, -2)
        return t + roll(t, 1, -2)

    c1_here, s1_here = halve([c_here, s_here])
    c1_here = COARSE_SCALE * c1_here
    cs1[0, H : H + X1, 0:Y1, :] = s1_here
    cs1[1, H : H + X1, 0:Y1, :] = c1_here
    copies_k = exchange(cs1, send_k, recv_k, H, X1, Y1, R1, H)
    four = flatten([COARSE_SCALE * c1_here, s1_here])
    row8 = iota((8, 128), 0)
    tile = four[0]
    for k in range(1, 4):
        tile = jnp.where(row8 % 4 == k, four[k], tile)
    cs2[DEEP + 1, pl.ds(me_l, 1)] = tile[None]
    copies_g = []
    for i, (dl, db) in enumerate(COLUMN):
        copy = pltpu.make_async_remote_copy(
            src_ref=cs2.at[DEEP + 1, pl.ds(me_l, 1)],
            dst_ref=cs2.at[DEEP + 1 - db, pl.ds(me_l, 1)],
            send_sem=send_g.at[i],
            recv_sem=recv_g.at[i],
            device_id=device(dl, db),
            device_id_type=MESH,
        )
        copy.start()
        copies_g.append(copy)

    def coefficients(buf, store, n_local, rows, y_local, step):
        mask3 = inside(n_local, 3, rows, y_local)
        n_f = buf.shape[0]
        c = jnp.where(mask3 > 0.5, buf[n_f - 1], 0.0)
        c_mid = c[1:-1]
        plus = smooth(c, step) + buf[n_f - 2, 1:-1]
        e = 8.0 * c_mid + plus
        g = DAMPING * mask3[1:-1] / (6.2 * c_mid + plus)
        store[0] = 1.0 - g * e
        store[1] = g * c_mid
        store[2] = g
        store[3] = c_mid
        store[4] = e
        buf[n_f - 1] = c

    arrive(copies_a)
    leave(copies_a)
    coefficients(raw, co0, X0, R0, Y0, 1)
    gain = co0[2]
    v1 = [gain * raw[k, 1:-1] for k in range(3)]
    for k in range(3):
        first0[k] = v1[k]
    c_12 = co0[3]
    inner = [co0[k, 1:-1] for k in range(3)]
    v2 = sweep(v1, c_12, None, inner, [f[1:-1] for f in v1], 1)
    for k in range(3):
        v2a[k, 2 : 2 + X0, 0:Y0, :] = v2[k][1:-1, :Y0]
    r0 = residual(
        v2, c_12[1:-1], co0[3, 2:-2, :Y0], co0[4, 2:-2, :Y0], [raw[k, H : H + X0, :Y0] for k in range(3)], 1, Y0
    )
    for k, f in enumerate(halve(r0)):
        b1[k, H : H + X1, 0:Y1, :] = f
    copies_b = exchange(b1, send_b, recv_b, 2, X1, Y1, R1, H)
    copies_v = exchange(v2a, send_v, recv_v, 2, X0, Y0, R0, 2)

    arrive(copies_g)
    copies_h = []
    for i, (dl, db) in enumerate(ROW):
        copy = pltpu.make_async_remote_copy(
            src_ref=cs2.at[:, pl.ds(me_l, 1)],
            dst_ref=cs2.at[:, pl.ds(me_l, 1)],
            send_sem=send_h.at[i],
            recv_sem=recv_h.at[i],
            device_id=device(dl, db),
            device_id_type=MESH,
        )
        copy.start()
        copies_h.append(copy)

    arrive(copies_k)
    leave(copies_k)
    coefficients(cs1, co1, X1, R1, Y1, 2)
    arrive(copies_b)
    gain = co1[2]
    v1 = [gain * b1[k, 1:-1] for k in range(3)]
    for k in range(3):
        first1[k] = v1[k]
    c_8 = co1[3]
    inner = [co1[k, 1:-1] for k in range(3)]
    v2 = sweep(v1, c_8, None, inner, [f[1:-1] for f in v1], 2)
    for k in range(3):
        v2b[k, H : H + X1, 0:Y1, :] = v2[k][1:-1, :Y1]
    r1 = residual(
        v2, c_8[1:-1], co1[3, 2:-2, :Y1], co1[4, 2:-2, :Y1], [b1[k, H : H + X1, :Y1] for k in range(3)], 2, Y1
    )
    six = flatten(r1)
    tile = jnp.where(row8 == 0, six[0], 0.0)
    for k in range(1, 6):
        tile = jnp.where(row8 == k, six[k], tile)
    sent2[0] = tile
    b2[pl.ds(DEEP * NL + me_l, 1)] = tile[None]
    for dl, db in FAR:
        pltpu.make_async_remote_copy(
            src_ref=sent2,
            dst_ref=b2.at[pl.ds((DEEP - db) * NL + me_l, 1)],
            send_sem=send_d.at[0],
            recv_sem=recv_d.at[0],
            device_id=device(dl, db),
            device_id_type=MESH,
        ).start()
    copies_w = exchange(v2b, send_w, recv_w, H, X1, Y1, R1, H)

    arrive(copies_h)
    leave(copies_h)
    leave(copies_g)
    leave(copies_b)
    leave(copies_v)
    u = cs2[...]
    w = roll(u, 2, -2)
    is_c = (row8 // 2) % 2 == 0
    valid = []
    for b in range(-DEEP - 1, DEEP + 2):
        ok = jnp.logical_and(me_b + b >= 0, me_b + b < NB)
        valid.append(jnp.broadcast_to(jnp.where(ok, one, zero), (1, 1, 8, 128)))
    valid = jnp.concatenate(valid, axis=0)
    c2 = jnp.where(is_c, u, w) * valid
    s2 = jnp.where(is_c, w, u)[1:-1]
    live = valid[1:-1] * jnp.where(row8 < 6, 1.0, 0.0).astype(F32)

    def deep_coefficients(c, smoothed, s, store):
        plus = smoothed + s
        e = 8.0 * c + plus
        g = DAMPING * live / (6.2 * c + plus)
        store[0] = 1.0 - g * e
        store[1] = g * c
        store[2] = g
        store[3] = c
        store[4] = e

    def restrict_deep(v):
        v = v + swap_pairs(v, 1, -2)
        v = v + swap_pairs(v, 32, -1)
        return 0.125 * (v + swap_pairs(v, 1, -1))

    deep_coefficients(c2[1:-1], smooth_deep(c2, 2, False), s2, co2)
    c3 = COARSE_SCALE * restrict_deep(c2[1:-1])
    deep_coefficients(c3, smooth_deep(c3, 3, True), restrict_deep(s2), co3)

    pltpu.make_async_copy(b2.at[pl.ds(0, len(FAR))], b2.at[pl.ds(0, len(FAR))], recv_d.at[0]).wait()

    def deep_sweep(v, store, tier, first, padded, lo, hi):
        mid = v if padded else v[1:-1]
        c = store[3, lo:hi] if padded else store[3, lo - 1 : hi + 1]
        drag = COUPLING * sum_deep(mid)
        return (
            store[0, lo:hi] * mid
            + first
            + store[1, lo:hi] * (smooth_deep(v, tier, padded) - drag)
            + store[2, lo:hi] * smooth_deep(c * v, tier, padded)
        )

    source = b2[...].reshape(GB, NL, 8, 128)
    v1 = co2[2] * source
    v2 = deep_sweep(v1, co2, 2, v1, True, 0, GB)
    c = co2[3]
    r2 = source - co2[4] * v2 + c * (smooth_deep(v2, 2, True) - COUPLING * sum_deep(v2)) + smooth_deep(c * v2, 2, True)
    f3 = co3[2] * restrict_deep(r2)
    v = deep_sweep(f3, co3, 3, f3[1:-1], False, 1, GB - 1)
    v = deep_sweep(v, co3, 3, f3[1:-1], True, 1, GB - 1)
    v = deep_sweep(v, co3, 3, f3[2:-2], False, 2, GB - 2)
    near = slice(DEEP - 1, DEEP + 2)
    v = v2[near] + v
    v = deep_sweep(v, co2, 2, v1[near], True, DEEP - 1, DEEP + 2)
    v = deep_sweep(v, co2, 2, v1[near], True, DEEP - 1, DEEP + 2)

    e2[:, 0:1] = jnp.zeros((3, 1, 8, 128), F32)
    e2[:, NL + 1 : NL + 2] = jnp.zeros((3, 1, 8, 128), F32)
    e2[:, 1 : NL + 1] = v
    rows72 = e2[:, pl.ds(me_l, 3)].reshape(72, 128)
    a, b = iota((128, 128), 0), iota((128, 128), 1)
    for y in range(4):
        spread = jnp.where(a == 32 * y + b // 4, 1.0, 0.0).astype(F32)
        pe2[y] = jnp.dot(rows72, spread, precision=lax.Precision.HIGHEST, preferred_element_type=F32)

    def coarse_rows(k, x2):
        group, parity = x2 // 2 + 1, x2 % 2

        def spread_row(brick, y):
            start = (brick * 3 + group) * 8 + k * 2 + parity
            return pe2[y, pl.ds(start, 8, stride=0), :]

        here = spread_row(1, 0)
        for y in range(1, 4):
            here = jnp.where(row8 // 2 == y, spread_row(1, y), here)
        halo = spread_row(2, 0)
        halo = jnp.where(row8 // 2 == 1, spread_row(2, 1), halo)
        halo = jnp.where(row8 // 2 == 2, spread_row(0, 2), halo)
        halo = jnp.where(row8 // 2 == 3, spread_row(0, 3), halo)
        return jnp.concatenate([here, halo], axis=0)

    up = []
    for k in range(3):
        cells = {x2: coarse_rows(k, x2) for x2 in range(-2, 4)}
        up.append(jnp.stack([cells[x // 2] for x in range(-H, X1 + H)], axis=0))
    arrive(copies_w)
    held = inside(X1, H, R1, Y1) > 0.5
    v = [jnp.where(held, v2b[k], 0.0) + up[k] for k in range(3)]
    v = sweep(v, cs1[1], None, [co1[k] for k in range(3)], [first1[k] for k in range(3)], 2)
    inner = [co1[k, 1:-1] for k in range(3)]
    v = sweep(v, co1[3], None, inner, [first1[k, 1:-1] for k in range(3)], 2)

    for k in range(3):
        pe1[k, :, pl.ds(0, Y1, stride=2), :] = v[k][:, :Y1]
        pe1[k, :, pl.ds(1, Y1, stride=2), :] = v[k][:, :Y1]
        t = v[k][:, Y1:]
        pe1[k, :, Y0:R0, :] = jnp.where(row8 == 1, roll(t, 1, -2), jnp.where(row8 == 6, roll(t, -1, -2), t))
    arrive(copies_v)
    up = []
    held = co0[2] > 0.0
    for k in range(3):
        e = pe1[k]
        up.append(jnp.where(held, v2a[k], 0.0) + jnp.broadcast_to(e[:, None], (6, 2, R0, 128)).reshape(12, R0, 128))
    c_12 = co0[3]
    v = sweep(up, c_12, None, [co0[k, 1:-1] for k in range(3)], [first0[k, 1:-1] for k in range(3)], 1)
    inner = [co0[k, 2:-2, :Y0] for k in range(3)]
    v = sweep(v, c_12[1:-1], None, inner, [first0[k, 2:-2, :Y0] for k in range(3)], 1, Y0)
    for k in range(3):
        out[k] = v[k]
    leave(copies_w)
    pltpu.make_async_copy(b2.at[pl.ds(0, len(FAR))], b2.at[pl.ds(0, len(FAR))], send_d.at[0]).wait()


def cycle(forces, modulus, occupancy, bonded):
    dma = pltpu.SemaphoreType.DMA
    vmem = pltpu.VMEM
    return pl.pallas_call(
        body,
        out_shape=jax.ShapeDtypeStruct((3, X0, Y0, 128), F32),
        in_specs=[pl.BlockSpec(memory_space=pl.ANY)] * 4,
        out_specs=pl.BlockSpec(memory_space=pltpu.VMEM),
        scratch_shapes=[
            vmem((5, X0 + 2 * H, R0, 128), F32),
            vmem((X0, Y0, 128), F32),
            vmem((X0, Y0, 128), jnp.int32),
            vmem((X0, Y0, 128), jnp.int32),
            vmem((2, X1 + 2 * H, R1, 128), F32),
            vmem((3, X1 + 2 * H, R1, 128), F32),
            vmem((3, X0 + 4, R0, 128), F32),
            vmem((3, X1 + 2 * H, R1, 128), F32),
            vmem((3, X0 + 4, R0, 128), F32),
            vmem((3, X1 + 4, R1, 128), F32),
            vmem((5, X0 + 4, R0, 128), F32),
            vmem((5, X1 + 4, R1, 128), F32),
            vmem((3, X1, Y0, 128), F32),
            vmem((GB + 2, NL, 8, 128), F32),
            vmem((GB * NL, 8, 128), F32),
            vmem((1, 8, 128), F32),
            vmem((5, GB, NL, 8, 128), F32),
            vmem((5, GB, NL, 8, 128), F32),
            vmem((3, NL + 2, 8, 128), F32),
            vmem((4, 72, 128), F32),
            vmem((3, 6, R0, 128), F32),
            dma((4,)),
            dma((8,)), dma((8,)), dma((8,)), dma((8,)), dma((8,)), dma((8,)), dma((8,)), dma((8,)), dma((8,)), dma((8,)),
            dma((len(COLUMN),)), dma((len(COLUMN),)), dma((len(ROW),)), dma((len(ROW),)), dma((1,)), dma((1,)),
        ],
        compiler_params=pltpu.CompilerParams(collective_id=0, has_side_effects=True, vmem_limit_bytes=48 << 20),
    )(forces, modulus, occupancy, bonded)


def solution(mesh):
    in_specs = (
        P(None, "len", "brick", None),
        P("len", "brick", None),
        P("len", "brick", None),
        P("len", "brick", None),
    )
    out_specs = P(None, "len", "brick", None)
    return jax.shard_map(cycle, mesh=mesh, in_specs=in_specs, out_specs=out_specs, check_vma=False)
```

```python
import functools

import jax
import jax.numpy as jnp
from jax import lax
from jax.experimental import pallas as pl
from jax.experimental.pallas import tpu as pltpu
from jax.sharding import PartitionSpec as P

DAMPING = 0.6
COUPLING = 0.2
MASS_TERM = 0.1
PENALTY = 20.0
COARSE_SCALE = 0.25

NL, NB = 8, 128
X0, Y0 = 8, 16
X1, Y1 = 4, 8
H = 3
R0, R1 = Y0 + 8, Y1 + 8
DEEP = 3
GB = 2 * DEEP + 1
MESH = pl.DeviceIdType.MESH
F32 = jnp.float32


def hops(dl, db):
    worst = 0
    for l in range(8):
        dx = abs((l + dl) % 8 // 2 - l // 2)
        for q in range(8):
            dy = abs((q + db) % 8 - q)
            worst = max(worst, min(dx, 4 - dx) + min(dy, 8 - dy) + abs((q + db) // 8))
    return worst


def far_first(pairs):
    return sorted(pairs, key=lambda p: -hops(*p))


NEAR = [(a, b) for b in (1, -1, 0) for a in (1, -1, 0) if (a, b) != (0, 0)]
FAR = [p for d in range(DEEP, -1, -1) for b in {d, -d} for p in far_first([(a, b) for a in range(-3, 5) if (a, b) != (0, 0)])]
COLUMN = far_first([(0, b) for b in range(-DEEP - 1, DEEP + 2) if b])
ROW = far_first([(a, 0) for a in range(-3, 5) if a])
GREETED = NEAR + [(4, 0), (4, 1), (4, -1)] + [p for p in COLUMN if p not in NEAR]


def iota(shape, dim):
    return lax.broadcasted_iota(jnp.int32, shape, dim)


def roll(x, shift, axis):
    size = x.shape[axis]
    return pltpu.roll(x, shift % size, axis % x.ndim)


def smooth_zy(v, step):
    rows = v.shape[-2]
    lane = iota((rows, 128), 1)
    low = jnp.where(lane >= step, 0.5, 0.0).astype(F32)
    high = jnp.where(lane < 128 - step, 0.5, 0.0).astype(F32)
    t = v + low * roll(v, step, -1) + high * roll(v, -step, -1)
    return t + 0.5 * (roll(t, 1, -2) + roll(t, -1, -2))


def smooth(v, step, rows=None):
    t = smooth_zy(v, step)
    if rows is not None:
        t = t[:, :rows]
    return t[1:-1] + 0.5 * (t[:-2] + t[2:])


def sweep(v, c, sides, coeffs, firsts, step, rows=None):
    keep, couple, gain = coeffs
    cut = slice(0, rows)
    mids = [f[1:-1, cut] for f in v]
    drag = COUPLING * (mids[0] + mids[1] + mids[2])
    return [
        keep * mids[k]
        + firsts[k]
        + couple * (smooth(v[k], step, rows) - drag)
        + gain * smooth(c * v[k], step, rows)
        for k in range(3)
    ]


def residual(v, c, c_mid, e_mid, source, step, rows):
    mids = [f[1:-1, :rows] for f in v]
    drag = COUPLING * (mids[0] + mids[1] + mids[2])
    return [
        source[k]
        - e_mid * mids[k]
        + c_mid * (smooth(v[k], step, rows) - drag)
        + smooth(c * v[k], step, rows)
        for k in range(3)
    ]


def swap_pairs(x, step, axis):
    index = iota(x.shape[-2:], 1 if axis in (-1, x.ndim - 1) else 0)
    return jnp.where((index // step) % 2 == 0, roll(x, -step, axis), roll(x, step, axis))


def shift_len(w, by):
    zero = jnp.zeros_like(w[:, :1])
    if by > 0:
        return jnp.concatenate([zero, w[:, :-1]], axis=1)
    return jnp.concatenate([w[:, 1:], zero], axis=1)


def neighbours_y(t, span, padded):
    lane = iota((8, 128), 1)
    up, down = roll(t, -span, -1), (roll(t, span, -1) if span != 64 else None)
    if down is None:
        down = up
    if padded:
        zero = jnp.zeros_like(t[:1])
        up_here, up_next = up, jnp.concatenate([up[1:], zero], axis=0)
        down_here, down_back = down, jnp.concatenate([zero, down[:-1]], axis=0)
    else:
        up_here, up_next = up[1:-1], up[2:]
        down_here, down_back = down[1:-1], down[:-2]
    return jnp.where(lane < 128 - span, up_here, up_next) + jnp.where(lane >= span, down_here, down_back)


def smooth_deep(v, tier, padded):
    step = 1 if tier == 2 else 2
    lane = iota((8, 128), 1)
    low = jnp.where(lane % 32 >= step, 0.5, 0.0).astype(F32)
    high = jnp.where(lane % 32 < 32 - step, 0.5, 0.0).astype(F32)
    t = v + low * roll(v, step, -1) + high * roll(v, -step, -1)
    mid = t if padded else t[1:-1]
    t = mid + 0.5 * neighbours_y(t, 32 if tier == 2 else 64, padded)
    if tier == 2:
        first = iota((8, 128), 0) % 2 == 0
        w = swap_pairs(t, 1, -2)
        beside = w + jnp.where(first, shift_len(w, 1), shift_len(w, -1))
    else:
        beside = shift_len(t, 1) + shift_len(t, -1)
    return t + 0.5 * beside


def sum_deep(v):
    u = v + roll(v, 2, -2)
    return u + roll(u, 4, -2)


def body(
    forces, modulus, occupancy, bonded, out, raw, mod_v, occ_v, bon_v, cs1, b1, v2a, v2b, first0, first1, co0, co1,
    pair, cs2, b2, sent2, co2, co3, e2, pe2, pe1,
    load_sem, send_a, recv_a, send_b, recv_b, send_k, recv_k, send_v, recv_v, send_w, recv_w,
    send_g, recv_g, send_h, recv_h, send_d, recv_d,
):
    me_l, me_b = lax.axis_index("len"), lax.axis_index("brick")

    def device(dl, db):
        return (lax.rem(me_l + dl + NL, NL), lax.rem(me_b + db + NB, NB))

    loads = [
        pltpu.make_async_copy(modulus, mod_v, load_sem.at[0]),
        pltpu.make_async_copy(occupancy, occ_v, load_sem.at[1]),
        pltpu.make_async_copy(bonded, bon_v, load_sem.at[2]),
        pltpu.make_async_copy(forces, raw.at[pl.ds(0, 3), pl.ds(H, X0), pl.ds(0, Y0), :], load_sem.at[3]),
    ]
    for load in loads:
        load.start()
    def exists(db):
        return jnp.logical_and(me_b + db >= 0, me_b + db < NB)

    def where_exists(db, act):
        if db == 0:
            act()
        else:
            pl.when(exists(db))(act)

    def by_brick(pairs):
        groups = {}
        for i, (dl, db) in enumerate(pairs):
            groups.setdefault(db, []).append((i, dl))
        return groups.items()

    barrier = pltpu.get_barrier_semaphore()
    for db, group in by_brick(GREETED):

        def greet(db=db, group=group):
            for _, dl in group:
                pl.semaphore_signal(barrier, inc=1, device_id=device(dl, db), device_id_type=MESH)

        where_exists(db, greet)

    def start(pairs, copies):
        for db, group in by_brick(pairs):

            def go(group=group):
                for i, _ in group:
                    copies[i].start()

            where_exists(db, go)

    def arrive(pairs, copies):
        for db, group in by_brick(pairs):

            def done(group=group):
                for i, _ in group:
                    copies[i].wait_recv()

            where_exists(-db, done)

    def leave(pairs, copies):
        for db, group in by_brick(pairs):

            def done(group=group):
                for i, _ in group:
                    copies[i].wait_send()

            where_exists(db, done)

    def exchange(buf, sends, recvs, width, size_x, size_y, rows, off):
        copies = []
        for i, (dl, db) in enumerate(NEAR):
            xs, xd, nx = {
                0: (off, off, size_x),
                1: (off + size_x - width, off - width, width),
                -1: (off, off + size_x, width),
            }[dl]
            ys, yd, ny = {
                0: (0, 0, size_y),
                1: (size_y - width, rows - width, width),
                -1: (0, size_y, width),
            }[db]
            copies.append(
                pltpu.make_async_remote_copy(
                    src_ref=buf.at[:, pl.ds(xs, nx), pl.ds(ys, ny), :],
                    dst_ref=buf.at[:, pl.ds(xd, nx), pl.ds(yd, ny), :],
                    send_sem=sends.at[i],
                    recv_sem=recvs.at[i],
                    device_id=device(dl, db),
                    device_id_type=MESH,
                )
            )
        start(NEAR, copies)
        return copies

    def clear(buf, rows, y_local):
        @pl.when(me_b == 0)
        def _():
            shape = buf.shape[:2] + (rows - y_local - 3, 128)
            buf[:, :, y_local + 3 :, :] = jnp.ones(shape, F32)

        @pl.when(me_b == NB - 1)
        def _():
            shape = buf.shape[:2] + (rows - y_local - 3, 128)
            buf[:, :, y_local : rows - 3, :] = jnp.ones(shape, F32)

    one, zero = jnp.float32(1.0), jnp.float32(0.0)
    low_x = jnp.where(me_l > 0, one, zero)
    high_x = jnp.where(me_l < NL - 1, one, zero)
    low_y = jnp.where(me_b > 0, one, zero)
    high_y = jnp.where(me_b < NB - 1, one, zero)

    def inside(n_local, halo, rows, y_local):
        row = iota((rows, 128), 0)
        in_y = jnp.where(row < y_local, one, jnp.where(row < y_local + 4, high_y, low_y))
        parts = [jnp.broadcast_to((in_y * low_x)[None], (halo, rows, 128))]
        parts.append(jnp.broadcast_to(in_y[None], (n_local, rows, 128)))
        parts.append(jnp.broadcast_to((in_y * high_x)[None], (halo, rows, 128)))
        return jnp.concatenate(parts, axis=0)

    for load in loads[:3]:
        load.wait()
    c_here = mod_v[...] * occ_v[...].astype(F32)
    s_here = MASS_TERM + PENALTY * bon_v[...].astype(F32)
    raw[3, H : H + X0, 0:Y0, :] = s_here
    raw[4, H : H + X0, 0:Y0, :] = c_here
    loads[3].wait()
    greeters = jnp.int32(0)
    for db, group in by_brick(GREETED):
        greeters = greeters + (len(group) if db == 0 else len(group) * exists(db).astype(jnp.int32))
    pl.semaphore_wait(barrier, greeters)
    copies_a = exchange(raw, send_a, recv_a, H, X0, Y0, R0, H)
    clear(raw, R0, Y0)
    clear(cs1, R1, Y1)
    clear(b1, R1, Y1)
    for db in range(-DEEP - 1, DEEP + 2):
        if db:

            @pl.when(jnp.logical_not(exists(db)))
            def _(db=db):
                cs2[DEEP + 1 + db, pl.ds(me_l, 1)] = jnp.ones((1, 8, 128), F32)
                if abs(db) <= DEEP:
                    b2[pl.ds((DEEP + db) * NL, NL)] = jnp.zeros((NL, 8, 128), F32)


    def halve(fields):
        result = []
        for k, f in enumerate(fields):
            f = f.reshape(X1, 2, Y0, 128)
            pair[k] = f[:, 0] + f[:, 1]
            u = pair[k, :, pl.ds(0, Y1, stride=2), :] + pair[k, :, pl.ds(1, Y1, stride=2), :]
            result.append(0.125 * (u + swap_pairs(u, 1, -1)))
        return result

    def flatten(fields):
        stacked = [f.reshape(2, 2, Y1, 128) for f in fields]
        stacked = jnp.concatenate([f[:, 0] + f[:, 1] for f in stacked], axis=0)
        n = stacked.shape[0]
        a, b = iota((128, 128), 0), iota((128, 128), 1)
        squeeze = jnp.where(a // 4 == b % 32, 0.0625, 0.0).astype(F32)
        t = jnp.dot(
            stacked.reshape(n * 8, 128), squeeze, precision=lax.Precision.HIGHEST, preferred_element_type=F32
        ).reshape(n, 8, 128)
        t = jnp.where(iota((8, 128), 1) // 32 == iota((8, 128), 0) // 2, t, 0.0)
        t = t + roll(t, 4, -2)
        t = t + roll(t, 2, -2)
        return t + roll(t, 1, -2)

    c1_here, s1_here = halve([c_here, s_here])
    c1_here = COARSE_SCALE * c1_here
    cs1[0, H : H + X1, 0:Y1, :] = s1_here
    cs1[1, H : H + X1, 0:Y1, :] = c1_here
    copies_k = exchange(cs1, send_k, recv_k, H, X1, Y1, R1, H)
    four = flatten([COARSE_SCALE * c1_here, s1_here])
    row8 = iota((8, 128), 0)
    tile = four[0]
    for k in range(1, 4):
        tile = jnp.where(row8 % 4 == k, four[k], tile)
    cs2[DEEP + 1, pl.ds(me_l, 1)] = tile[None]
    copies_g = []
    for i, (dl, db) in enumerate(COLUMN):
        copy = pltpu.make_async_remote_copy(
            src_ref=cs2.at[DEEP + 1, pl.ds(me_l, 1)],
            dst_ref=cs2.at[DEEP + 1 - db, pl.ds(me_l, 1)],
            send_sem=send_g.at[i],
            recv_sem=recv_g.at[i],
            device_id=device(dl, db),
            device_id_type=MESH,
        )
        copies_g.append(copy)
    start(COLUMN, copies_g)

    def coefficients(buf, store, n_local, rows, y_local, step):
        mask3 = inside(n_local, 3, rows, y_local)
        n_f = buf.shape[0]
        c = jnp.where(mask3 > 0.5, buf[n_f - 1], 0.0)
        c_mid = c[1:-1]
        plus = smooth(c, step) + buf[n_f - 2, 1:-1]
        e = 8.0 * c_mid + plus
        g = DAMPING * mask3[1:-1] / (6.2 * c_mid + plus)
        store[0] = 1.0 - g * e
        store[1] = g * c_mid
        store[2] = g
        store[3] = c_mid
        store[4] = e
        buf[n_f - 1] = c

    arrive(NEAR, copies_a)
    leave(NEAR, copies_a)
    coefficients(raw, co0, X0, R0, Y0, 1)
    gain = co0[2]
    v1 = [gain * raw[k, 1:-1] for k in range(3)]
    for k in range(3):
        first0[k] = v1[k]
    c_12 = co0[3]
    inner = [co0[k, 1:-1] for k in range(3)]
    v2 = sweep(v1, c_12, None, inner, [f[1:-1] for f in v1], 1)
    for k in range(3):
        v2a[k, 2 : 2 + X0, 0:Y0, :] = v2[k][1:-1, :Y0]
    r0 = residual(
        v2, c_12[1:-1], co0[3, 2:-2, :Y0], co0[4, 2:-2, :Y0], [raw[k, H : H + X0, :Y0] for k in range(3)], 1, Y0
    )
    for k, f in enumerate(halve(r0)):
        b1[k, H : H + X1, 0:Y1, :] = f
    copies_b = exchange(b1, send_b, recv_b, 2, X1, Y1, R1, H)
    copies_v = exchange(v2a, send_v, recv_v, 2, X0, Y0, R0, 2)

    arrive(COLUMN, copies_g)
    copies_h = []
    for i, (dl, db) in enumerate(ROW):
        copy = pltpu.make_async_remote_copy(
            src_ref=cs2.at[:, pl.ds(me_l, 1)],
            dst_ref=cs2.at[:, pl.ds(me_l, 1)],
            send_sem=send_h.at[i],
            recv_sem=recv_h.at[i],
            device_id=device(dl, db),
            device_id_type=MESH,
        )
        copies_h.append(copy)
    start(ROW, copies_h)

    arrive(NEAR, copies_k)
    leave(NEAR, copies_k)
    coefficients(cs1, co1, X1, R1, Y1, 2)
    arrive(NEAR, copies_b)
    gain = co1[2]
    v1 = [gain * b1[k, 1:-1] for k in range(3)]
    for k in range(3):
        first1[k] = v1[k]
    c_8 = co1[3]
    inner = [co1[k, 1:-1] for k in range(3)]
    v2 = sweep(v1, c_8, None, inner, [f[1:-1] for f in v1], 2)
    for k in range(3):
        v2b[k, H : H + X1, 0:Y1, :] = v2[k][1:-1, :Y1]
    r1 = residual(
        v2, c_8[1:-1], co1[3, 2:-2, :Y1], co1[4, 2:-2, :Y1], [b1[k, H : H + X1, :Y1] for k in range(3)], 2, Y1
    )
    six = flatten(r1)
    tile = jnp.where(row8 == 0, six[0], 0.0)
    for k in range(1, 6):
        tile = jnp.where(row8 == k, six[k], tile)
    sent2[0] = tile
    b2[pl.ds(DEEP * NL + me_l, 1)] = tile[None]
    for db, group in by_brick(FAR):

        def spread(db=db, group=group):
            for _, dl in group:
                pltpu.make_async_remote_copy(
                    src_ref=sent2,
                    dst_ref=b2.at[pl.ds((DEEP - db) * NL + me_l, 1)],
                    send_sem=send_d.at[DEEP + db],
                    recv_sem=recv_d.at[DEEP - db],
                    device_id=device(dl, db),
                    device_id_type=MESH,
                ).start()

        where_exists(db, spread)

    def await_far(sems):
        for db, group in by_brick(FAR):

            def done(db=db, count=len(group)):
                held = b2.at[pl.ds(0, count)]
                pltpu.make_async_copy(held, held, sems.at[DEEP + db]).wait()

            where_exists(db, done)

    copies_w = exchange(v2b, send_w, recv_w, H, X1, Y1, R1, H)

    arrive(ROW, copies_h)
    leave(ROW, copies_h)
    leave(COLUMN, copies_g)
    leave(NEAR, copies_b)
    leave(NEAR, copies_v)
    u = cs2[...]
    w = roll(u, 2, -2)
    is_c = (row8 // 2) % 2 == 0
    valid = []
    for b in range(-DEEP - 1, DEEP + 2):
        valid.append(jnp.broadcast_to(jnp.where(exists(b), one, zero), (1, 1, 8, 128)))
    valid = jnp.concatenate(valid, axis=0)
    c2 = jnp.where(is_c, u, w) * valid
    s2 = jnp.where(is_c, w, u)[1:-1]
    live = valid[1:-1] * jnp.where(row8 < 6, 1.0, 0.0).astype(F32)

    def deep_coefficients(c, smoothed, s, store):
        plus = smoothed + s
        e = 8.0 * c + plus
        g = DAMPING * live / (6.2 * c + plus)
        store[0] = 1.0 - g * e
        store[1] = g * c
        store[2] = g
        store[3] = c
        store[4] = e

    def restrict_deep(v):
        v = v + swap_pairs(v, 1, -2)
        v = v + swap_pairs(v, 32, -1)
        return 0.125 * (v + swap_pairs(v, 1, -1))

    deep_coefficients(c2[1:-1], smooth_deep(c2, 2, False), s2, co2)
    c3 = COARSE_SCALE * restrict_deep(c2[1:-1])
    deep_coefficients(c3, smooth_deep(c3, 3, True), restrict_deep(s2), co3)

    await_far(recv_d)

    def deep_sweep(v, store, tier, first, padded, lo, hi):
        mid = v if padded else v[1:-1]
        c = store[3, lo:hi] if padded else store[3, lo - 1 : hi + 1]
        drag = COUPLING * sum_deep(mid)
        return (
            store[0, lo:hi] * mid
            + first
            + store[1, lo:hi] * (smooth_deep(v, tier, padded) - drag)
            + store[2, lo:hi] * smooth_deep(c * v, tier, padded)
        )

    source = b2[...].reshape(GB, NL, 8, 128)
    v1 = co2[2] * source
    v2 = deep_sweep(v1, co2, 2, v1, True, 0, GB)
    c = co2[3]
    r2 = source - co2[4] * v2 + c * (smooth_deep(v2, 2, True) - COUPLING * sum_deep(v2)) + smooth_deep(c * v2, 2, True)
    f3 = co3[2] * restrict_deep(r2)
    v = deep_sweep(f3, co3, 3, f3[1:-1], False, 1, GB - 1)
    v = deep_sweep(v, co3, 3, f3[1:-1], True, 1, GB - 1)
    v = deep_sweep(v, co3, 3, f3[2:-2], False, 2, GB - 2)
    near = slice(DEEP - 1, DEEP + 2)
    v = v2[near] + v
    v = deep_sweep(v, co2, 2, v1[near], True, DEEP - 1, DEEP + 2)
    v = deep_sweep(v, co2, 2, v1[near], True, DEEP - 1, DEEP + 2)

    e2[:, 0:1] = jnp.zeros((3, 1, 8, 128), F32)
    e2[:, NL + 1 : NL + 2] = jnp.zeros((3, 1, 8, 128), F32)
    e2[:, 1 : NL + 1] = v
    rows72 = e2[:, pl.ds(me_l, 3)].reshape(72, 128)
    a, b = iota((128, 128), 0), iota((128, 128), 1)
    for y in range(4):
        spread = jnp.where(a == 32 * y + b // 4, 1.0, 0.0).astype(F32)
        pe2[y] = jnp.dot(rows72, spread, precision=lax.Precision.HIGHEST, preferred_element_type=F32)

    def coarse_rows(k, x2):
        group, parity = x2 // 2 + 1, x2 % 2

        def spread_row(brick, y):
            start = (brick * 3 + group) * 8 + k * 2 + parity
            return pe2[y, pl.ds(start, 8, stride=0), :]

        here = spread_row(1, 0)
        for y in range(1, 4):
            here = jnp.where(row8 // 2 == y, spread_row(1, y), here)
        halo = spread_row(2, 0)
        halo = jnp.where(row8 // 2 == 1, spread_row(2, 1), halo)
        halo = jnp.where(row8 // 2 == 2, spread_row(0, 2), halo)
        halo = jnp.where(row8 // 2 == 3, spread_row(0, 3), halo)
        return jnp.concatenate([here, halo], axis=0)

    up = []
    for k in range(3):
        cells = {x2: coarse_rows(k, x2) for x2 in range(-2, 4)}
        up.append(jnp.stack([cells[x // 2] for x in range(-H, X1 + H)], axis=0))
    arrive(NEAR, copies_w)
    held = inside(X1, H, R1, Y1) > 0.5
    v = [jnp.where(held, v2b[k], 0.0) + up[k] for k in range(3)]
    v = sweep(v, cs1[1], None, [co1[k] for k in range(3)], [first1[k] for k in range(3)], 2)
    inner = [co1[k, 1:-1] for k in range(3)]
    v = sweep(v, co1[3], None, inner, [first1[k, 1:-1] for k in range(3)], 2)

    for k in range(3):
        pe1[k, :, pl.ds(0, Y1, stride=2), :] = v[k][:, :Y1]
        pe1[k, :, pl.ds(1, Y1, stride=2), :] = v[k][:, :Y1]
        t = v[k][:, Y1:]
        pe1[k, :, Y0:R0, :] = jnp.where(row8 == 1, roll(t, 1, -2), jnp.where(row8 == 6, roll(t, -1, -2), t))
    arrive(NEAR, copies_v)
    up = []
    held = co0[2] > 0.0
    for k in range(3):
        e = pe1[k]
        up.append(jnp.where(held, v2a[k], 0.0) + jnp.broadcast_to(e[:, None], (6, 2, R0, 128)).reshape(12, R0, 128))
    c_12 = co0[3]
    v = sweep(up, c_12, None, [co0[k, 1:-1] for k in range(3)], [first0[k, 1:-1] for k in range(3)], 1)
    inner = [co0[k, 2:-2, :Y0] for k in range(3)]
    v = sweep(v, c_12[1:-1], None, inner, [first0[k, 2:-2, :Y0] for k in range(3)], 1, Y0)
    for k in range(3):
        out[k] = v[k]
    leave(NEAR, copies_w)
    await_far(send_d)


def cycle(forces, modulus, occupancy, bonded):
    dma = pltpu.SemaphoreType.DMA
    vmem = pltpu.VMEM
    return pl.pallas_call(
        body,
        out_shape=jax.ShapeDtypeStruct((3, X0, Y0, 128), F32),
        in_specs=[pl.BlockSpec(memory_space=pl.ANY)] * 4,
        out_specs=pl.BlockSpec(memory_space=pltpu.VMEM),
        scratch_shapes=[
            vmem((5, X0 + 2 * H, R0, 128), F32),
            vmem((X0, Y0, 128), F32),
            vmem((X0, Y0, 128), jnp.int32),
            vmem((X0, Y0, 128), jnp.int32),
            vmem((2, X1 + 2 * H, R1, 128), F32),
            vmem((3, X1 + 2 * H, R1, 128), F32),
            vmem((3, X0 + 4, R0, 128), F32),
            vmem((3, X1 + 2 * H, R1, 128), F32),
            vmem((3, X0 + 4, R0, 128), F32),
            vmem((3, X1 + 4, R1, 128), F32),
            vmem((5, X0 + 4, R0, 128), F32),
            vmem((5, X1 + 4, R1, 128), F32),
            vmem((3, X1, Y0, 128), F32),
            vmem((GB + 2, NL, 8, 128), F32),
            vmem((GB * NL, 8, 128), F32),
            vmem((1, 8, 128), F32),
            vmem((5, GB, NL, 8, 128), F32),
            vmem((5, GB, NL, 8, 128), F32),
            vmem((3, NL + 2, 8, 128), F32),
            vmem((4, 72, 128), F32),
            vmem((3, 6, R0, 128), F32),
            dma((4,)),
            dma((8,)), dma((8,)), dma((8,)), dma((8,)), dma((8,)), dma((8,)), dma((8,)), dma((8,)), dma((8,)), dma((8,)),
            dma((len(COLUMN),)), dma((len(COLUMN),)), dma((len(ROW),)), dma((len(ROW),)), dma((GB,)), dma((GB,)),
        ],
        compiler_params=pltpu.CompilerParams(collective_id=0, has_side_effects=True, vmem_limit_bytes=56 << 20),
    )(forces, modulus, occupancy, bonded)


def solution(mesh):
    in_specs = (
        P(None, "len", "brick", None),
        P("len", "brick", None),
        P("len", "brick", None),
        P("len", "brick", None),
    )
    out_specs = P(None, "len", "brick", None)
    return jax.shard_map(cycle, mesh=mesh, in_specs=in_specs, out_specs=out_specs, check_vma=False)
```

```python
import functools

import jax
import jax.numpy as jnp
from jax import lax
from jax.experimental import pallas as pl
from jax.experimental.pallas import tpu as pltpu
from jax.sharding import PartitionSpec as P

DAMPING = 0.6
COUPLING = 0.2
MASS_TERM = 0.1
PENALTY = 20.0
COARSE_SCALE = 0.25

NL, NB = 8, 128
X0, Y0 = 8, 16
X1, Y1 = 4, 8
H = 3
R0, R1 = Y0 + 8, Y1 + 8
DEEP = 3
GB = 2 * DEEP + 1
MESH = pl.DeviceIdType.MESH
F32 = jnp.float32


def hops(dl, db):
    worst = 0
    for l in range(8):
        dx = abs((l + dl) % 8 // 2 - l // 2)
        for q in range(8):
            dy = abs((q + db) % 8 - q)
            worst = max(worst, min(dx, 4 - dx) + min(dy, 8 - dy) + abs((q + db) // 8))
    return worst


def far_first(pairs):
    return sorted(pairs, key=lambda p: -hops(*p))


NEAR = [(a, b) for b in (1, -1, 0) for a in (1, -1, 0) if (a, b) != (0, 0)]
FAR = [p for d in range(DEEP, -1, -1) for b in {d, -d} for p in far_first([(a, b) for a in range(-3, 5) if (a, b) != (0, 0)])]
COLUMN = far_first([(0, b) for b in range(-DEEP - 1, DEEP + 2) if b])
ROW = far_first([(a, 0) for a in range(-3, 5) if a])
GREETED = NEAR + [(4, 0), (4, 1), (4, -1)] + [p for p in COLUMN if p not in NEAR]


def iota(shape, dim):
    return lax.broadcasted_iota(jnp.int32, shape, dim)


def roll(x, shift, axis):
    size = x.shape[axis]
    return pltpu.roll(x, shift % size, axis % x.ndim)


def smooth_zy(v, step):
    rows = v.shape[-2]
    lane = iota((rows, 128), 1)
    low = jnp.where(lane >= step, 0.5, 0.0).astype(F32)
    high = jnp.where(lane < 128 - step, 0.5, 0.0).astype(F32)
    t = v + low * roll(v, step, -1) + high * roll(v, -step, -1)
    return t + 0.5 * (roll(t, 1, -2) + roll(t, -1, -2))


def smooth(v, step, rows=None):
    t = smooth_zy(v, step)
    if rows is not None:
        t = t[:, :rows]
    return t[1:-1] + 0.5 * (t[:-2] + t[2:])


def sweep(v, c, sides, coeffs, firsts, step, rows=None):
    keep, couple, gain = coeffs
    cut = slice(0, rows)
    mids = [f[1:-1, cut] for f in v]
    drag = COUPLING * (mids[0] + mids[1] + mids[2])
    return [
        keep * mids[k]
        + firsts[k]
        + couple * (smooth(v[k], step, rows) - drag)
        + gain * smooth(c * v[k], step, rows)
        for k in range(3)
    ]


def residual(v, c, c_mid, e_mid, source, step, rows):
    mids = [f[1:-1, :rows] for f in v]
    drag = COUPLING * (mids[0] + mids[1] + mids[2])
    return [
        source[k]
        - e_mid * mids[k]
        + c_mid * (smooth(v[k], step, rows) - drag)
        + smooth(c * v[k], step, rows)
        for k in range(3)
    ]


def swap_pairs(x, step, axis):
    index = iota(x.shape[-2:], 1 if axis in (-1, x.ndim - 1) else 0)
    return jnp.where((index // step) % 2 == 0, roll(x, -step, axis), roll(x, step, axis))


def shift_len(w, by):
    zero = jnp.zeros_like(w[:, :1])
    if by > 0:
        return jnp.concatenate([zero, w[:, :-1]], axis=1)
    return jnp.concatenate([w[:, 1:], zero], axis=1)


def neighbours_y(t, span, padded):
    lane = iota((8, 128), 1)
    up, down = roll(t, -span, -1), (roll(t, span, -1) if span != 64 else None)
    if down is None:
        down = up
    if padded:
        zero = jnp.zeros_like(t[:1])
        up_here, up_next = up, jnp.concatenate([up[1:], zero], axis=0)
        down_here, down_back = down, jnp.concatenate([zero, down[:-1]], axis=0)
    else:
        up_here, up_next = up[1:-1], up[2:]
        down_here, down_back = down[1:-1], down[:-2]
    return jnp.where(lane < 128 - span, up_here, up_next) + jnp.where(lane >= span, down_here, down_back)


def smooth_deep(v, tier, padded):
    step = 1 if tier == 2 else 2
    lane = iota((8, 128), 1)
    low = jnp.where(lane % 32 >= step, 0.5, 0.0).astype(F32)
    high = jnp.where(lane % 32 < 32 - step, 0.5, 0.0).astype(F32)
    t = v + low * roll(v, step, -1) + high * roll(v, -step, -1)
    mid = t if padded else t[1:-1]
    t = mid + 0.5 * neighbours_y(t, 32 if tier == 2 else 64, padded)
    if tier == 2:
        first = iota((8, 128), 0) % 2 == 0
        w = swap_pairs(t, 1, -2)
        beside = w + jnp.where(first, shift_len(w, 1), shift_len(w, -1))
    else:
        beside = shift_len(t, 1) + shift_len(t, -1)
    return t + 0.5 * beside


def sum_deep(v):
    u = v + roll(v, 2, -2)
    return u + roll(u, 4, -2)


def body(
    forces, modulus, occupancy, bonded, out, raw, mod_v, occ_v, bon_v, cs1, b1, v2a, v2b, first0, first1, co0, co1,
    pair, cs2, b2, sent2, co2, co3, e2, pe2, pe1,
    load_sem, send_c, recv_c, send_a, recv_a, send_b, recv_b, send_k, recv_k, send_v, recv_v, send_w, recv_w,
    send_g, recv_g, send_h, recv_h, send_d, recv_d,
):
    me_l, me_b = lax.axis_index("len"), lax.axis_index("brick")

    def device(dl, db):
        at = me_l + dl
        if dl > 0:
            at = jnp.where(at >= NL, at - NL, at)
        elif dl < 0:
            at = jnp.where(at < 0, at + NL, at)
        return (at, me_b + db)

    loads = [
        pltpu.make_async_copy(modulus, mod_v, load_sem.at[0]),
        pltpu.make_async_copy(occupancy, occ_v, load_sem.at[1]),
        pltpu.make_async_copy(bonded, bon_v, load_sem.at[2]),
        pltpu.make_async_copy(forces, raw.at[pl.ds(0, 3), pl.ds(H, X0), pl.ds(0, Y0), :], load_sem.at[3]),
    ]
    def exists(db):
        return jnp.logical_and(me_b + db >= 0, me_b + db < NB)

    def where_exists(db, act):
        if db == 0:
            act()
        else:
            pl.when(exists(db))(act)

    def by_brick(pairs):
        groups = {}
        for i, (dl, db) in enumerate(pairs):
            groups.setdefault(db, []).append((i, dl))
        return groups.items()

    barrier = pltpu.get_barrier_semaphore()
    for db, group in by_brick(GREETED):

        def greet(db=db, group=group):
            for _, dl in group:
                pl.semaphore_signal(barrier, inc=1, device_id=device(dl, db), device_id_type=MESH)

        where_exists(db, greet)
    for load in loads:
        load.start()

    def start(pairs, copies):
        for db, group in by_brick(pairs):

            def go(group=group):
                for i, _ in group:
                    copies[i].start()

            where_exists(db, go)

    def arrive(pairs, copies):
        for db, group in by_brick(pairs):

            def done(group=group):
                for i, _ in group:
                    copies[i].wait_recv()

            where_exists(-db, done)

    def leave(pairs, copies):
        for db, group in by_brick(pairs):

            def done(group=group):
                for i, _ in group:
                    copies[i].wait_send()

            where_exists(db, done)

    def exchange(buf, sends, recvs, width, size_x, size_y, rows, off, low=0, count=None):
        fields = pl.ds(low, buf.shape[0] if count is None else count)
        copies = []
        for i, (dl, db) in enumerate(NEAR):
            xs, xd, nx = {
                0: (off, off, size_x),
                1: (off + size_x - width, off - width, width),
                -1: (off, off + size_x, width),
            }[dl]
            ys, yd, ny = {
                0: (0, 0, size_y),
                1: (size_y - width, rows - width, width),
                -1: (0, size_y, width),
            }[db]
            copies.append(
                pltpu.make_async_remote_copy(
                    src_ref=buf.at[fields, pl.ds(xs, nx), pl.ds(ys, ny), :],
                    dst_ref=buf.at[fields, pl.ds(xd, nx), pl.ds(yd, ny), :],
                    send_sem=sends.at[i],
                    recv_sem=recvs.at[i],
                    device_id=device(dl, db),
                    device_id_type=MESH,
                )
            )
        start(NEAR, copies)
        return copies

    def clear(buf, rows, y_local):
        @pl.when(me_b == 0)
        def _():
            shape = buf.shape[:2] + (rows - y_local - 3, 128)
            buf[:, :, y_local + 3 :, :] = jnp.ones(shape, F32)

        @pl.when(me_b == NB - 1)
        def _():
            shape = buf.shape[:2] + (rows - y_local - 3, 128)
            buf[:, :, y_local : rows - 3, :] = jnp.ones(shape, F32)

    one, zero = jnp.float32(1.0), jnp.float32(0.0)
    low_x = jnp.where(me_l > 0, one, zero)
    high_x = jnp.where(me_l < NL - 1, one, zero)
    low_y = jnp.where(me_b > 0, one, zero)
    high_y = jnp.where(me_b < NB - 1, one, zero)

    def inside(n_local, halo, rows, y_local):
        row = iota((rows, 128), 0)
        in_y = jnp.where(row < y_local, one, jnp.where(row < y_local + 4, high_y, low_y))
        parts = [jnp.broadcast_to((in_y * low_x)[None], (halo, rows, 128))]
        parts.append(jnp.broadcast_to(in_y[None], (n_local, rows, 128)))
        parts.append(jnp.broadcast_to((in_y * high_x)[None], (halo, rows, 128)))
        return jnp.concatenate(parts, axis=0)

    for load in loads[:3]:
        load.wait()
    c_here = mod_v[...] * occ_v[...].astype(F32)
    s_here = MASS_TERM + PENALTY * bon_v[...].astype(F32)
    raw[3, H : H + X0, 0:Y0, :] = s_here
    raw[4, H : H + X0, 0:Y0, :] = c_here
    loads[3].wait()
    greeters = jnp.int32(0)
    for db, group in by_brick(GREETED):
        greeters = greeters + (len(group) if db == 0 else len(group) * exists(db).astype(jnp.int32))
    pl.semaphore_wait(barrier, greeters)
    copies_c = exchange(raw, send_c, recv_c, H, X0, Y0, R0, H, 4, 1)
    copies_a = exchange(raw, send_a, recv_a, 2, X0, Y0, R0, H, 0, 4)
    clear(raw, R0, Y0)
    clear(cs1, R1, Y1)
    clear(b1, R1, Y1)
    for db in range(-DEEP - 1, DEEP + 2):
        if db:

            @pl.when(jnp.logical_not(exists(db)))
            def _(db=db):
                cs2[DEEP + 1 + db, pl.ds(me_l, 1)] = jnp.ones((1, 8, 128), F32)
                if abs(db) <= DEEP:
                    b2[pl.ds((DEEP + db) * NL, NL)] = jnp.zeros((NL, 8, 128), F32)


    def halve(fields):
        result = []
        for k, f in enumerate(fields):
            f = f.reshape(X1, 2, Y0, 128)
            pair[k] = f[:, 0] + f[:, 1]
            u = pair[k, :, pl.ds(0, Y1, stride=2), :] + pair[k, :, pl.ds(1, Y1, stride=2), :]
            result.append(0.125 * (u + swap_pairs(u, 1, -1)))
        return result

    def flatten(fields):
        stacked = [f.reshape(2, 2, Y1, 128) for f in fields]
        stacked = jnp.concatenate([f[:, 0] + f[:, 1] for f in stacked], axis=0)
        n = stacked.shape[0]
        a, b = iota((128, 128), 0), iota((128, 128), 1)
        squeeze = jnp.where(a // 4 == b % 32, 0.0625, 0.0).astype(F32)
        t = jnp.dot(
            stacked.reshape(n * 8, 128), squeeze, precision=lax.Precision.HIGHEST, preferred_element_type=F32
        ).reshape(n, 8, 128)
        t = jnp.where(iota((8, 128), 1) // 32 == iota((8, 128), 0) // 2, t, 0.0)
        t = t + roll(t, 4, -2)
        t = t + roll(t, 2, -2)
        return t + roll(t, 1, -2)

    c1_here, s1_here = halve([c_here, s_here])
    c1_here = COARSE_SCALE * c1_here
    cs1[0, H : H + X1, 0:Y1, :] = s1_here
    cs1[1, H : H + X1, 0:Y1, :] = c1_here
    copies_k = exchange(cs1, send_k, recv_k, H, X1, Y1, R1, H)
    four = flatten([COARSE_SCALE * c1_here, s1_here])
    row8 = iota((8, 128), 0)
    tile = four[0]
    for k in range(1, 4):
        tile = jnp.where(row8 % 4 == k, four[k], tile)
    cs2[DEEP + 1, pl.ds(me_l, 1)] = tile[None]
    copies_g = []
    for i, (dl, db) in enumerate(COLUMN):
        copy = pltpu.make_async_remote_copy(
            src_ref=cs2.at[DEEP + 1, pl.ds(me_l, 1)],
            dst_ref=cs2.at[DEEP + 1 - db, pl.ds(me_l, 1)],
            send_sem=send_g.at[i],
            recv_sem=recv_g.at[i],
            device_id=device(dl, db),
            device_id_type=MESH,
        )
        copies_g.append(copy)
    start(COLUMN, copies_g)

    def coefficients(buf, store, n_local, rows, y_local, step):
        mask3 = inside(n_local, 3, rows, y_local)
        n_f = buf.shape[0]
        c = jnp.where(mask3 > 0.5, buf[n_f - 1], 0.0)
        c_mid = c[1:-1]
        plus = smooth(c, step) + buf[n_f - 2, 1:-1]
        e = 8.0 * c_mid + plus
        g = DAMPING * mask3[1:-1] / (6.2 * c_mid + plus)
        store[0] = 1.0 - g * e
        store[1] = g * c_mid
        store[2] = g
        store[3] = c_mid
        store[4] = e
        buf[n_f - 1] = c

    arrive(NEAR, copies_c)
    leave(NEAR, copies_c)
    arrive(NEAR, copies_a)
    leave(NEAR, copies_a)
    coefficients(raw, co0, X0, R0, Y0, 1)
    gain = co0[2]
    v1 = [gain * raw[k, 1:-1] for k in range(3)]
    for k in range(3):
        first0[k] = v1[k]
    c_12 = co0[3]
    inner = [co0[k, 1:-1] for k in range(3)]
    v2 = sweep(v1, c_12, None, inner, [f[1:-1] for f in v1], 1)
    for k in range(3):
        v2a[k, 2 : 2 + X0, 0:Y0, :] = v2[k][1:-1, :Y0]
    r0 = residual(
        v2, c_12[1:-1], co0[3, 2:-2, :Y0], co0[4, 2:-2, :Y0], [raw[k, H : H + X0, :Y0] for k in range(3)], 1, Y0
    )
    for k, f in enumerate(halve(r0)):
        b1[k, H : H + X1, 0:Y1, :] = f
    copies_b = exchange(b1, send_b, recv_b, 2, X1, Y1, R1, H)
    copies_v = exchange(v2a, send_v, recv_v, 2, X0, Y0, R0, 2)

    arrive(COLUMN, copies_g)
    copies_h = []
    for i, (dl, db) in enumerate(ROW):
        copy = pltpu.make_async_remote_copy(
            src_ref=cs2.at[:, pl.ds(me_l, 1)],
            dst_ref=cs2.at[:, pl.ds(me_l, 1)],
            send_sem=send_h.at[i],
            recv_sem=recv_h.at[i],
            device_id=device(dl, db),
            device_id_type=MESH,
        )
        copies_h.append(copy)
    start(ROW, copies_h)

    arrive(NEAR, copies_k)
    leave(NEAR, copies_k)
    coefficients(cs1, co1, X1, R1, Y1, 2)
    arrive(NEAR, copies_b)
    gain = co1[2]
    v1 = [gain * b1[k, 1:-1] for k in range(3)]
    for k in range(3):
        first1[k] = v1[k]
    c_8 = co1[3]
    inner = [co1[k, 1:-1] for k in range(3)]
    v2 = sweep(v1, c_8, None, inner, [f[1:-1] for f in v1], 2)
    for k in range(3):
        v2b[k, H : H + X1, 0:Y1, :] = v2[k][1:-1, :Y1]
    r1 = residual(
        v2, c_8[1:-1], co1[3, 2:-2, :Y1], co1[4, 2:-2, :Y1], [b1[k, H : H + X1, :Y1] for k in range(3)], 2, Y1
    )
    six = flatten(r1)
    tile = jnp.where(row8 == 0, six[0], 0.0)
    for k in range(1, 6):
        tile = jnp.where(row8 == k, six[k], tile)
    sent2[0] = tile
    b2[pl.ds(DEEP * NL + me_l, 1)] = tile[None]
    for db, group in by_brick(FAR):

        def spread(db=db, group=group):
            for _, dl in group:
                pltpu.make_async_remote_copy(
                    src_ref=sent2.at[:, pl.ds(0, 6)],
                    dst_ref=b2.at[pl.ds((DEEP - db) * NL + me_l, 1), pl.ds(0, 6)],
                    send_sem=send_d.at[DEEP + db],
                    recv_sem=recv_d.at[DEEP - db],
                    device_id=device(dl, db),
                    device_id_type=MESH,
                ).start()

        where_exists(db, spread)

    def await_far(sems):
        for db, group in by_brick(FAR):

            def done(db=db, count=len(group)):
                held = b2.at[pl.ds(0, count), pl.ds(0, 6)]
                pltpu.make_async_copy(held, held, sems.at[DEEP + db]).wait()

            where_exists(db, done)

    copies_w = exchange(v2b, send_w, recv_w, H, X1, Y1, R1, H)

    arrive(ROW, copies_h)
    leave(ROW, copies_h)
    leave(COLUMN, copies_g)
    leave(NEAR, copies_b)
    leave(NEAR, copies_v)
    u = cs2[...]
    w = roll(u, 2, -2)
    is_c = (row8 // 2) % 2 == 0
    valid = []
    for b in range(-DEEP - 1, DEEP + 2):
        valid.append(jnp.broadcast_to(jnp.where(exists(b), one, zero), (1, 1, 8, 128)))
    valid = jnp.concatenate(valid, axis=0)
    c2 = jnp.where(is_c, u, w) * valid
    s2 = jnp.where(is_c, w, u)[1:-1]
    live = valid[1:-1] * jnp.where(row8 < 6, 1.0, 0.0).astype(F32)

    def deep_coefficients(c, smoothed, s, store):
        plus = smoothed + s
        e = 8.0 * c + plus
        g = DAMPING * live / (6.2 * c + plus)
        store[0] = 1.0 - g * e
        store[1] = g * c
        store[2] = g
        store[3] = c
        store[4] = e

    def restrict_deep(v):
        v = v + swap_pairs(v, 1, -2)
        v = v + swap_pairs(v, 32, -1)
        return 0.125 * (v + swap_pairs(v, 1, -1))

    deep_coefficients(c2[1:-1], smooth_deep(c2, 2, False), s2, co2)
    c3 = COARSE_SCALE * restrict_deep(c2[1:-1])
    deep_coefficients(c3, smooth_deep(c3, 3, True), restrict_deep(s2), co3)

    leave(NEAR, copies_w)
    await_far(send_d)
    arrive(NEAR, copies_v)
    await_far(recv_d)

    def deep_sweep(v, store, tier, first, padded, lo, hi):
        mid = v if padded else v[1:-1]
        c = store[3, lo:hi] if padded else store[3, lo - 1 : hi + 1]
        drag = COUPLING * sum_deep(mid)
        return (
            store[0, lo:hi] * mid
            + first
            + store[1, lo:hi] * (smooth_deep(v, tier, padded) - drag)
            + store[2, lo:hi] * smooth_deep(c * v, tier, padded)
        )

    source = jnp.where(row8 < 6, b2[...], 0.0).reshape(GB, NL, 8, 128)
    v1 = co2[2] * source
    v2 = deep_sweep(v1, co2, 2, v1, True, 0, GB)
    c = co2[3]
    r2 = source - co2[4] * v2 + c * (smooth_deep(v2, 2, True) - COUPLING * sum_deep(v2)) + smooth_deep(c * v2, 2, True)
    f3 = co3[2] * restrict_deep(r2)
    v = deep_sweep(f3, co3, 3, f3[1:-1], False, 1, GB - 1)
    v = deep_sweep(v, co3, 3, f3[1:-1], True, 1, GB - 1)
    v = deep_sweep(v, co3, 3, f3[2:-2], False, 2, GB - 2)
    near = slice(DEEP - 1, DEEP + 2)
    v = v2[near] + v
    v = deep_sweep(v, co2, 2, v1[near], True, DEEP - 1, DEEP + 2)
    v = deep_sweep(v, co2, 2, v1[near], True, DEEP - 1, DEEP + 2)

    e2[:, 0:1] = jnp.zeros((3, 1, 8, 128), F32)
    e2[:, NL + 1 : NL + 2] = jnp.zeros((3, 1, 8, 128), F32)
    e2[:, 1 : NL + 1] = v
    rows72 = e2[:, pl.ds(me_l, 3)].reshape(72, 128)
    a, b = iota((128, 128), 0), iota((128, 128), 1)
    for y in range(4):
        spread = jnp.where(a == 32 * y + b // 4, 1.0, 0.0).astype(F32)
        pe2[y] = jnp.dot(rows72, spread, precision=lax.Precision.HIGHEST, preferred_element_type=F32)

    def coarse_rows(k, x2):
        group, parity = x2 // 2 + 1, x2 % 2

        def spread_row(brick, y):
            start = (brick * 3 + group) * 8 + k * 2 + parity
            return pe2[y, pl.ds(start, 8, stride=0), :]

        here = spread_row(1, 0)
        for y in range(1, 4):
            here = jnp.where(row8 // 2 == y, spread_row(1, y), here)
        halo = spread_row(2, 0)
        halo = jnp.where(row8 // 2 == 1, spread_row(2, 1), halo)
        halo = jnp.where(row8 // 2 == 2, spread_row(0, 2), halo)
        halo = jnp.where(row8 // 2 == 3, spread_row(0, 3), halo)
        return jnp.concatenate([here, halo], axis=0)

    up = []
    for k in range(3):
        cells = {x2: coarse_rows(k, x2) for x2 in range(-2, 4)}
        up.append(jnp.stack([cells[x // 2] for x in range(-H, X1 + H)], axis=0))
    arrive(NEAR, copies_w)
    held = inside(X1, H, R1, Y1) > 0.5
    v = [jnp.where(held, v2b[k], 0.0) + up[k] for k in range(3)]
    v = sweep(v, cs1[1], None, [co1[k] for k in range(3)], [first1[k] for k in range(3)], 2)
    inner = [co1[k, 1:-1] for k in range(3)]
    v = sweep(v, co1[3], None, inner, [first1[k, 1:-1] for k in range(3)], 2)

    for k in range(3):
        pe1[k, :, pl.ds(0, Y1, stride=2), :] = v[k][:, :Y1]
        pe1[k, :, pl.ds(1, Y1, stride=2), :] = v[k][:, :Y1]
        t = v[k][:, Y1:]
        pe1[k, :, Y0:R0, :] = jnp.where(row8 == 1, roll(t, 1, -2), jnp.where(row8 == 6, roll(t, -1, -2), t))
    up = []
    held = co0[2] > 0.0
    for k in range(3):
        e = pe1[k]
        up.append(jnp.where(held, v2a[k], 0.0) + jnp.broadcast_to(e[:, None], (6, 2, R0, 128)).reshape(12, R0, 128))
    c_12 = co0[3]
    v = sweep(up, c_12, None, [co0[k, 1:-1] for k in range(3)], [first0[k, 1:-1] for k in range(3)], 1)
    inner = [co0[k, 2:-2, :Y0] for k in range(3)]
    v = sweep(v, c_12[1:-1], None, inner, [first0[k, 2:-2, :Y0] for k in range(3)], 1, Y0)
    for k in range(3):
        out[k] = v[k]


def cycle(forces, modulus, occupancy, bonded):
    dma = pltpu.SemaphoreType.DMA
    vmem = pltpu.VMEM
    return pl.pallas_call(
        body,
        out_shape=jax.ShapeDtypeStruct((3, X0, Y0, 128), F32),
        in_specs=[pl.BlockSpec(memory_space=pl.ANY)] * 4,
        out_specs=pl.BlockSpec(memory_space=pltpu.VMEM),
        scratch_shapes=[
            vmem((5, X0 + 2 * H, R0, 128), F32),
            vmem((X0, Y0, 128), F32),
            vmem((X0, Y0, 128), jnp.int32),
            vmem((X0, Y0, 128), jnp.int32),
            vmem((2, X1 + 2 * H, R1, 128), F32),
            vmem((3, X1 + 2 * H, R1, 128), F32),
            vmem((3, X0 + 4, R0, 128), F32),
            vmem((3, X1 + 2 * H, R1, 128), F32),
            vmem((3, X0 + 4, R0, 128), F32),
            vmem((3, X1 + 4, R1, 128), F32),
            vmem((5, X0 + 4, R0, 128), F32),
            vmem((5, X1 + 4, R1, 128), F32),
            vmem((3, X1, Y0, 128), F32),
            vmem((GB + 2, NL, 8, 128), F32),
            vmem((GB * NL, 8, 128), F32),
            vmem((1, 8, 128), F32),
            vmem((5, GB, NL, 8, 128), F32),
            vmem((5, GB, NL, 8, 128), F32),
            vmem((3, NL + 2, 8, 128), F32),
            vmem((4, 72, 128), F32),
            vmem((3, 6, R0, 128), F32),
            dma((4,)),
            dma((8,)), dma((8,)), dma((8,)), dma((8,)), dma((8,)), dma((8,)), dma((8,)), dma((8,)), dma((8,)), dma((8,)),
            dma((8,)), dma((8,)),
            dma((len(COLUMN),)), dma((len(COLUMN),)), dma((len(ROW),)), dma((len(ROW),)), dma((GB,)), dma((GB,)),
        ],
        compiler_params=pltpu.CompilerParams(collective_id=0, has_side_effects=True, vmem_limit_bytes=56 << 20),
    )(forces, modulus, occupancy, bonded)


def solution(mesh):
    in_specs = (
        P(None, "len", "brick", None),
        P("len", "brick", None),
        P("len", "brick", None),
        P("len", "brick", None),
    )
    out_specs = P(None, "len", "brick", None)
    return jax.shard_map(cycle, mesh=mesh, in_specs=in_specs, out_specs=out_specs, check_vma=False)
```
